512 devices in a mesh: replica: 8 (over z_lo), shard: 64 (over z_hi, x, y, core).
Axes of the slice: x: 4, y: 4, z: 16 (z_hi: 2, z_lo: 8; z = z_hi * 8 + z_lo), core: 2. Of those that a mesh axis runs over, the one named last changes fastest.
Arguments:
- pseudo_grads: bfloat16 [8, 2, 5120, 5120], P('replica', None, 'shard'), may hold values from -400 to 400
- momentum: float32 [2, 5120, 5120], P(None, 'shard', 'replica'), may hold values from -3 to 3
Outputs:
- update: bfloat16 [2, 5120, 5120], P(None, 'shard')
- momentum_next: float32 [2, 5120, 5120], P(None, 'shard', 'replica')
The draws below stay inside these ranges and needn't reach their ends.
All inputs are finite; a program needn't handle non-finite values.
Results may differ from the reference program's by a relative error of at most 0.015.
Values may be sent and summed in bfloat16 or wider, within the bound.
A program may use at most 64 MiB of HBM per device.

```python
import math
import jax
import jax.numpy as jnp
from jax import lax

D = 5120
HD = 5120
LAYERS = 2
ITERS = 5
BLOCK = 80
N_REPLICA = 8


def draw_pseudo_grads(key, part):
    shape = (N_REPLICA, LAYERS, D, HD)
    gaussian = jnp.clip(jax.random.normal(key, shape, jnp.float32), -6.0, 6.0)
    row_rise = 1.0 + 2.0 * jnp.arange(D, dtype=jnp.float32) / D
    col_rise = 1.0 + 2.0 * jnp.arange(HD, dtype=jnp.float32) / HD
    rising = row_rise[None, None, :, None] * col_rise[None, None, None, :]
    values = gaussian * rising * 0.5
    return values.astype(jnp.bfloat16)


def steps_of(stream_key, shape, shards, low, largest):
    loudness = 1.0
    for axis_at, parts in shards:
        draws = jax.random.uniform(jax.random.fold_in(jax.random.fold_in(stream_key, 6), axis_at), (parts,), jnp.float32, low / len(shards), largest / len(shards))
        loudness = loudness * jnp.repeat(jnp.exp(draws), shape[axis_at] // parts).reshape((-1,) + (1,) * (len(shape) - 1 - axis_at))
    return loudness


def centred(rng, shape, width, limit, cuts=(), held_as=jnp.bfloat16):
    values = jax.random.normal(rng, shape, jnp.float32) * width
    if len(cuts) > 0:
        values = steps_of(rng, shape, cuts, -0.22, 0.18) * values
    return jnp.clip(values, min=-limit, max=limit).astype(held_as)


def setup_inputs(seed: int = 0) -> dict:
    streams_of = jax.random.split(jax.random.key(seed), 3)
    return {
        "pseudo_grads": draw_pseudo_grads(jax.random.fold_in(streams_of[2], 71), 0),
        "momentum": centred(streams_of[1], (LAYERS, D, HD), 0.5, 3.0, ((1, 64), (2, 8)), jnp.float32),
    }


QUINTIC_FIRST = 3.4445
QUINTIC_SECOND = -4.775
QUINTIC_THIRD = 2.0315
MOMENTUM_RATE = 0.9
EPSILON = 1e-07
EXACTNESS = lax.Precision.HIGHEST

def polish(blocks):
    gram_matrix = jnp.einsum('lbik,lbjk->lbij', blocks, blocks, precision=EXACTNESS)
    mixture = QUINTIC_SECOND * gram_matrix + QUINTIC_THIRD * jnp.einsum('lbij,lbjk->lbik', gram_matrix, gram_matrix, precision=EXACTNESS)
    return QUINTIC_FIRST * blocks + jnp.einsum('lbij,lbjk->lbik', mixture, blocks, precision=EXACTNESS)

def reference(pseudo_grads, momentum):

    def accumulate(running, replica_grad):
        return (running + replica_grad.astype(jnp.float32), None)
    running, _ = lax.scan(accumulate, jnp.zeros(pseudo_grads.shape[1:], jnp.float32), pseudo_grads)
    average = running / N_REPLICA
    momentum_next = MOMENTUM_RATE * momentum + average
    direction = average + MOMENTUM_RATE * momentum_next
    frobenius = jnp.sqrt(lax.optimization_barrier(jnp.sum(direction * direction, axis=(1, 2))))
    factor = 1.0 / (frobenius + EPSILON)
    blocks = (direction * factor[:, None, None]).reshape(LAYERS, D // BLOCK, BLOCK, HD)
    for iteration in range(ITERS):
        blocks = polish(blocks)
    update = (blocks * math.sqrt(HD)).reshape(LAYERS, D, HD).astype(jnp.bfloat16)
    return (update, momentum_next)
```

```python
import functools
import math

import jax
import jax.numpy as jnp
from jax import lax
from jax.experimental import pallas as pl
from jax.experimental.pallas import tpu as pltpu
from jax.sharding import PartitionSpec as P

ITERS = 5
QUINTIC_FIRST = 3.4445
QUINTIC_SECOND = -4.775
QUINTIC_THIRD = 2.0315
MOMENTUM_RATE = 0.9
EPSILON = 1e-07
EXACTNESS = lax.Precision.HIGHEST
MESH = pl.DeviceIdType.MESH

SHARD_AXES = (2, 4, 4, 2)
TILE = 128
LAG = 5


def kernel(
    n, axes, grads_hbm, moment_hbm, out_hbm, next_hbm,
    grads, moment, fresh, gathered, right_part, left_part, gram, squares, plane_in, ring_in, result,
    load_sem, right_recv, left_recv, gather_recv, right_send, left_send, gather_right, gather_left,
    plane_send, plane_recv, ring_send, ring_recv, token_up, token_down, store_sem,
):
    halves, xs, ys, cores = axes
    layers, rows, cols = grads.shape
    width = cols // n
    per_layer = width // TILE
    slices = layers * per_layer
    last = n - 1
    ring = halves * n

    i = lax.axis_index("replica")
    shard = lax.axis_index("shard")
    core = lax.rem(shard, cores)
    y = lax.rem(lax.div(shard, cores), ys)
    x = lax.rem(lax.div(shard, cores * ys), xs)
    half = lax.div(shard, cores * ys * xs)
    z = half * n + i
    in_plane = shard - half * (cores * ys * xs)

    def along_z(offset):
        there = lax.rem(z + offset, ring)
        return (lax.rem(there, n), lax.div(there, n) * (cores * ys * xs) + in_plane)

    def along_x(offset):
        there = lax.rem(x + offset, xs)
        return (i, ((half * xs + there) * ys + y) * cores + core)

    def along_y(offset):
        there = lax.rem(y + offset, ys)
        return (i, ((half * xs + x) * ys + there) * cores + core)

    def along_core(offset):
        there = lax.rem(core + offset, cores)
        return (i, ((half * xs + x) * ys + y) * cores + there)

    stages = [(along_x, xs), (along_y, ys), (along_core, cores)]
    stages = [s for s in stages if s[1] > 1]
    right, left = (i + 1, shard), (i - 1, shard)
    up, down = along_z(1), along_z(ring - 1)

    loads = [
        pltpu.make_async_copy(grads_hbm.at[0], grads, load_sem.at[0]),
        pltpu.make_async_copy(moment_hbm, moment, load_sem.at[1]),
    ]
    for load in loads:
        load.start()

    barrier = pltpu.get_barrier_semaphore()
    friends = [up, down]
    for where, size in stages:
        friends += [where(offset) for offset in range(1, size)]
    for friend in friends:
        pl.semaphore_signal(barrier, inc=1, device_id=friend, device_id_type=MESH)

    gram[...] = jnp.zeros_like(gram)
    squares[...] = jnp.zeros_like(squares)
    for s in range(slices):
        right_part[s, 0] = jnp.zeros((rows, TILE), jnp.bfloat16)
        left_part[s, last] = jnp.zeros((rows, TILE), jnp.bfloat16)
    for load in loads:
        load.wait()
    pl.semaphore_wait(barrier, len(friends))

    def columns(s, j):
        return pl.ds(pl.multiple_of(j * width + lax.rem(s, per_layer) * TILE, TILE), TILE)

    def layer(s):
        return lax.div(s, per_layer)

    def part_copy(part, s, j, send, recv, target):
        return pltpu.make_async_remote_copy(
            src_ref=part.at[s, j], dst_ref=part.at[s, j], send_sem=send.at[s, j], recv_sem=recv.at[s, j],
            device_id=target, device_id_type=MESH)

    def chunk_copy(s, c, send, target):
        chunk = gathered.at[layer(s), :, columns(s, c)]
        return pltpu.make_async_remote_copy(
            src_ref=chunk, dst_ref=chunk, send_sem=send.at[s, c], recv_sem=gather_recv.at[s, c],
            device_id=target, device_id_type=MESH)

    def hop(part, s, j, send, recv, target, first):
        own = grads.at[layer(s), :, columns(s, j)]

        @pl.when(i == first)
        def _():
            pltpu.make_async_remote_copy(
                src_ref=own, dst_ref=part.at[s, j], send_sem=send.at[s, j], recv_sem=recv.at[s, j],
                device_id=target, device_id_type=MESH).start()

        @pl.when(i != first)
        def _():
            copy = part_copy(part, s, j, send, recv, target)
            copy.wait_recv()
            total = part[s, j].astype(jnp.float32) + own[...].astype(jnp.float32)
            part[s, j] = total.astype(jnp.bfloat16)
            copy.start()

    upper = lax.div(i, n // 2)
    far = upper * i + (1 - upper) * (last - i)
    final_at = last - far + far * LAG
    closing = (slices - 1) * last + final_at

    def finish(s):
        @pl.when(i > 0)
        def _():
            part_copy(right_part, s, i, right_send, right_recv, right).wait_recv()

        @pl.when(i < last)
        def _():
            part_copy(left_part, s, i, left_send, left_recv, left).wait_recv()

        k = layer(s)
        here = pl.ds(pl.multiple_of(lax.rem(s, per_layer) * TILE, TILE), TILE)
        total = (
            grads[k, :, columns(s, i)].astype(jnp.float32)
            + right_part[s, i].astype(jnp.float32)
            + left_part[s, i].astype(jnp.float32)
        )
        average = total / n
        moment_next = MOMENTUM_RATE * moment[k, :, here] + average
        direction = average + MOMENTUM_RATE * moment_next
        fresh[k, :, here] = moment_next
        gathered[k, :, columns(s, i)] = direction.astype(jnp.bfloat16)
        row_sum = jnp.sum(direction * direction, axis=0, keepdims=True)
        squares[0, pl.ds(k, 1), :] += row_sum

        @pl.when(i < last)
        def _():
            chunk_copy(s, i, gather_right, right).start()

        @pl.when(i > 0)
        def _():
            chunk_copy(s, i, gather_left, left).start()

    def exchange(stage):
        where, size = stages[stage]
        return [
            pltpu.make_async_remote_copy(
                src_ref=squares.at[stage], dst_ref=plane_in.at[stage, offset], send_sem=plane_send.at[stage, offset],
                recv_sem=plane_recv.at[stage, offset], device_id=where(offset), device_id_type=MESH)
            for offset in range(1, size)
        ]

    def add_up(stage):
        total = squares[stage]
        for offset, copy in enumerate(exchange(stage), 1):
            copy.wait_recv()
            total = total + plane_in[stage, offset]
        squares[stage + 1] = total

    def around(offset):
        return pltpu.make_async_remote_copy(
            src_ref=squares.at[len(stages)], dst_ref=ring_in.at[offset], send_sem=ring_send.at[offset],
            recv_sem=ring_recv.at[offset], device_id=along_z(offset), device_id_type=MESH)

    def tick(t, carry):
        @pl.when((lax.rem(t, 4) == 0) & (t < 2 * ring))
        def _():
            pl.semaphore_signal(token_up, inc=1, device_id=up, device_id_type=MESH)
            pl.semaphore_signal(token_down, inc=1, device_id=down, device_id_type=MESH)
            pl.semaphore_wait(token_up, 1)
            pl.semaphore_wait(token_down, 1)

        to_right = t - i * LAG
        @pl.when((to_right >= 0) & (to_right < last * slices))
        def _():
            s, j = lax.div(to_right, last), last - lax.rem(to_right, last)
            @pl.when(i < j)
            def _():
                hop(right_part, s, j, right_send, right_recv, right, 0)

        to_left = t - (last - i) * LAG
        @pl.when((to_left >= 0) & (to_left < last * slices))
        def _():
            s, j = lax.div(to_left, last), lax.rem(to_left, last)
            @pl.when(i > j)
            def _():
                hop(left_part, s, j, left_send, left_recv, left, last)

        since = t - final_at
        @pl.when((since >= 0) & (since < last * slices))
        def _():
            @pl.when(lax.rem(since, last) == 0)
            def _():
                finish(lax.div(since, last))

        @pl.when(t == closing)
        def _():
            pltpu.make_async_copy(fresh, next_hbm, store_sem.at[0]).start()
            if stages:
                for copy in exchange(0):
                    copy.start()

        for stage in range(len(stages)):
            @pl.when(t == closing + 5 * (stage + 1))
            def _():
                add_up(stage)
                if stage + 1 < len(stages):
                    for copy in exchange(stage + 1):
                        copy.start()

        @pl.when(t == closing + 5 * len(stages))
        def _():
            for offset in range(1, ring):
                around(offset).start()

        for c in reversed(range(last)):
            if c >= n // 2:
                due = last - c + i * LAG
            else:
                due = c + (last + i - 2 * c) * LAG
            late = t - due
            @pl.when((c < i) & (late >= 0) & (late < last * slices))
            def _():
                @pl.when(lax.rem(late, last) == 0)
                def _():
                    copy = chunk_copy(lax.div(late, last), c, gather_right, right)
                    copy.wait_recv()
                    @pl.when(i < last)
                    def _():
                        copy.start()

        for back in reversed(range(last)):
            c = last - back
            if back >= n // 2:
                due = last - back + (last - i) * LAG
            else:
                due = back + (last + last - i - 2 * back) * LAG
            late = t - due
            @pl.when((c > i) & (late >= 0) & (late < last * slices))
            def _():
                @pl.when(lax.rem(late, last) == 0)
                def _():
                    copy = chunk_copy(lax.div(late, last), c, gather_left, left)
                    copy.wait_recv()
                    @pl.when(i > 0)
                    def _():
                        copy.start()

        whole = t - (last + far) * LAG - 1
        @pl.when((whole >= 0) & (whole < last * slices))
        def _():
            @pl.when(lax.rem(whole, last) == 0)
            def _():
                s = lax.div(whole, last)
                k = layer(s)
                band = jnp.concatenate([gathered[k, :, columns(s, c)] for c in range(n)], axis=1)
                gram[k] += lax.dot_general(
                    band, band, (((1,), (1,)), ((), ())), preferred_element_type=jnp.float32)

        return carry

    ticks = (slices - 1) * last + 2 * last * LAG + 2
    lax.fori_loop(0, ticks, tick, 0)

    total = squares[len(stages)]
    for offset in range(1, ring):
        around(offset).wait_recv()
        total = total + ring_in[offset]

    eye = (lax.broadcasted_iota(jnp.int32, (rows, rows), 0) == lax.broadcasted_iota(jnp.int32, (rows, rows), 1))
    eye = eye.astype(jnp.float32)
    product = functools.partial(jnp.dot, precision=EXACTNESS, preferred_element_type=jnp.float32)
    factors, states, mixes = [], [], []
    for k in range(layers):
        norm = jnp.sqrt(jnp.sum(total[k : k + 1, :], axis=1, keepdims=True))
        factor = 1.0 / (norm + EPSILON)
        factors.append(factor)
        states.append(gram[k] * (factor * factor))
        mixes.append(None)
    for step in range(ITERS):
        for k in range(layers):
            state = states[k]
            square = product(state, state)
            poly = QUINTIC_FIRST * eye + QUINTIC_SECOND * state + QUINTIC_THIRD * square
            mixes[k] = poly if mixes[k] is None else product(poly, mixes[k])
            if step + 1 < ITERS:
                states[k] = product(product(state, poly), poly)

    span = cols // 4
    for k in range(layers):
        mix = mixes[k] * (factors[k] * math.sqrt(cols))
        high = mix.astype(jnp.bfloat16)
        low = (mix - high.astype(jnp.float32)).astype(jnp.bfloat16)
        for at in range(cols // span):
            window = pl.ds(at * span, span)
            block = gathered[k, :, window]
            value = jnp.dot(high, block, preferred_element_type=jnp.float32)
            value = value + jnp.dot(low, block, preferred_element_type=jnp.float32)
            result[k, :, window] = value.astype(jnp.bfloat16)
            pltpu.make_async_copy(
                result.at[k, :, window], out_hbm.at[k, :, window], store_sem.at[1 + k * (cols // span) + at]).start()

    def drain(s, carry):
        for j in range(n):
            if j > 0:
                @pl.when(i < j)
                def _():
                    part_copy(right_part, s, j, right_send, right_recv, right).wait_send()
            if j < last:
                @pl.when(i > j)
                def _():
                    part_copy(left_part, s, j, left_send, left_recv, left).wait_send()
            @pl.when((i < last) & (j <= i))
            def _():
                chunk_copy(s, j, gather_right, right).wait_send()
            @pl.when((i > 0) & (j >= i))
            def _():
                chunk_copy(s, j, gather_left, left).wait_send()
        return carry

    lax.fori_loop(0, slices, drain, 0)
    for stage in range(len(stages)):
        for copy in exchange(stage):
            copy.wait_send()
    for offset in range(1, ring):
        around(offset).wait_send()
    pltpu.make_async_copy(fresh, next_hbm, store_sem.at[0]).wait()
    for k in range(layers):
        for at in range(cols // span):
            window = pl.ds(at * span, span)
            pltpu.make_async_copy(
                result.at[k, :, window], out_hbm.at[k, :, window], store_sem.at[1 + k * (cols // span) + at]).wait()


def body(axes, pseudo_grads, momentum):
    n = lax.axis_size("replica")
    _, layers, rows, cols = pseudo_grads.shape
    width = cols // n
    slices = layers * width // TILE
    ring = axes[0] * n
    dma = pltpu.SemaphoreType.DMA
    any_spec = pl.BlockSpec(memory_space=pl.ANY)
    bf16, f32 = jnp.bfloat16, jnp.float32
    return pl.pallas_call(
        functools.partial(kernel, n, axes),
        out_shape=(
            jax.ShapeDtypeStruct((layers, rows, cols), bf16),
            jax.ShapeDtypeStruct((layers, rows, width), f32),
        ),
        in_specs=[any_spec, any_spec],
        out_specs=(any_spec, any_spec),
        scratch_shapes=[
            pltpu.VMEM((layers, rows, cols), bf16),
            pltpu.VMEM((layers, rows, width), f32),
            pltpu.VMEM((layers, rows, width), f32),
            pltpu.VMEM((layers, rows, cols), bf16),
            pltpu.VMEM((slices, n, rows, TILE), bf16),
            pltpu.VMEM((slices, n, rows, TILE), bf16),
            pltpu.VMEM((layers, rows, rows), f32),
            pltpu.VMEM((4, 8, TILE), f32),
            pltpu.VMEM((3, 4, 8, TILE), f32),
            pltpu.VMEM((ring, 8, TILE), f32),
            pltpu.VMEM((layers, rows, cols), bf16),
            dma((2,)),
            dma((slices, n)),
            dma((slices, n)),
            dma((slices, n)),
            dma((slices, n)),
            dma((slices, n)),
            dma((slices, n)),
            dma((slices, n)),
            dma((3, 4)),
            dma((3, 4)),
            dma((ring,)),
            dma((ring,)),
            pltpu.SemaphoreType.REGULAR,
            pltpu.SemaphoreType.REGULAR,
            dma((16,)),
        ],
        compiler_params=pltpu.CompilerParams(
            collective_id=0, has_side_effects=True, vmem_limit_bytes=40 * 1024 * 1024),
    )(pseudo_grads, momentum)


def solution(mesh, axes=SHARD_AXES):
    placed = (P("replica", None, "shard", None), P(None, "shard", "replica"))
    return jax.shard_map(
        functools.partial(body, axes),
        mesh=mesh,
        in_specs=placed,
        out_specs=(P(None, "shard", None), P(None, "shard", "replica")),
        check_vma=False,
    )
```

```python
import functools
import math

import jax
import jax.numpy as jnp
from jax import lax
from jax.experimental import pallas as pl
from jax.experimental.pallas import tpu as pltpu
from jax.sharding import PartitionSpec as P

ITERS = 5
QUINTIC_FIRST = 3.4445
QUINTIC_SECOND = -4.775
QUINTIC_THIRD = 2.0315
MOMENTUM_RATE = 0.9
EPSILON = 1e-07
EXACTNESS = lax.Precision.HIGHEST
MESH = pl.DeviceIdType.MESH

SHARD_AXES = (2, 4, 4, 2)
TILE = 128
GROUP = 8
LAG = 9


def kernel(
    n, axes, grads_hbm, moment_hbm, out_hbm, next_hbm,
    grads, moment, fresh, gathered, inward_part, cross_part, gram, squares, plane_in, ring_in, result,
    load_sem, inward_recv, cross_recv, outward_recv, inward_send, outward_send,
    plane_send, plane_recv, ring_send, ring_recv, store_sem,
):
    halves, xs, ys, cores = axes
    layers, rows, cols = grads.shape
    width = cols // n
    per_layer = cols // TILE
    messages = layers * per_layer
    ring = halves * n
    middle = n // 2 - 1

    gain = (1.0 + MOMENTUM_RATE) / n
    mixed = MOMENTUM_RATE * MOMENTUM_RATE / gain

    i = lax.axis_index("replica")
    shard = lax.axis_index("shard")
    core = lax.rem(shard, cores)
    y = lax.rem(lax.div(shard, cores), ys)
    x = lax.rem(lax.div(shard, cores * ys), xs)
    half = lax.div(shard, cores * ys * xs)
    z = half * n + i
    in_plane = shard - half * (cores * ys * xs)
    upper = lax.div(i, n // 2)
    depth = i + upper * (n - 1 - 2 * i)
    inward = (i + 1 - 2 * upper, shard)
    outward = (i - 1 + 2 * upper, shard)

    def along_z(offset):
        there = lax.rem(z + offset, ring)
        return (lax.rem(there, n), lax.div(there, n) * (cores * ys * xs) + in_plane)

    offsets = [(a, b, c) for a in range(xs) for b in range(ys) for c in range(cores)][1:]

    def across(a, b, c):
        there = (lax.rem(x + a, xs) * ys + lax.rem(y + b, ys)) * cores + lax.rem(core + c, cores)
        return (i, half * (cores * ys * xs) + there)

    up, down = along_z(1), along_z(ring - 1)

    loads = [
        pltpu.make_async_copy(moment_hbm, moment, load_sem.at[0]),
        pltpu.make_async_copy(grads_hbm.at[0], grads, load_sem.at[1]),
    ]
    for load in loads:
        load.start()

    barrier = pltpu.get_barrier_semaphore()
    for friend in (up, down):
        pl.semaphore_signal(barrier, inc=1, device_id=friend, device_id_type=MESH)

    if halves > 1:
        far = (n // 2 - upper, lax.rem(half + 1, halves) * (cores * ys * xs) + in_plane)
        pl.semaphore_signal(barrier, inc=1, device_id=far, device_id_type=MESH)

    @pl.when(depth == middle)
    def _():
        for offset in offsets:
            pl.semaphore_signal(barrier, inc=1, device_id=across(*offset), device_id_type=MESH)

    gram[...] = jnp.zeros_like(gram)
    squares[...] = jnp.zeros_like(squares)
    for load in loads:
        load.wait()
    mine = pl.ds(pl.multiple_of(i * width, TILE), width)
    for k in range(layers):
        own = grads[k, :, mine].astype(jnp.float32) + mixed * moment[k]
        grads[k, :, mine] = own.astype(jnp.bfloat16)

    @pl.when(depth == middle)
    def _():
        pl.semaphore_wait(barrier, 2 + len(offsets) + (halves - 1) * (n // 2))

    @pl.when(depth != middle)
    def _():
        pl.semaphore_wait(barrier, 2)

    def place(ref, m):
        column = pl.multiple_of(lax.rem(m, per_layer) * TILE, TILE)
        return ref.at[lax.div(m, per_layer), :, pl.ds(column, TILE)]

    def inward_copy(m, source):
        return pltpu.make_async_remote_copy(
            src_ref=source, dst_ref=inward_part.at[m], send_sem=inward_send.at[m], recv_sem=inward_recv.at[m],
            device_id=inward, device_id_type=MESH)

    def cross_copy(m):
        return pltpu.make_async_remote_copy(
            src_ref=inward_part.at[m], dst_ref=cross_part.at[m], send_sem=inward_send.at[m],
            recv_sem=cross_recv.at[m], device_id=inward, device_id_type=MESH)

    def outward_copy(m):
        chunk = place(gathered, m)
        return pltpu.make_async_remote_copy(
            src_ref=chunk, dst_ref=chunk, send_sem=outward_send.at[m], recv_sem=outward_recv.at[m],
            device_id=outward, device_id_type=MESH)

    def send_inward(m):
        own = place(grads, m)

        @pl.when(depth == 0)
        def _():
            inward_copy(m, own).start()

        @pl.when(depth > 0)
        def _():
            inward_copy(m, own).wait_recv()
            total = inward_part[m].astype(jnp.float32) + own[...].astype(jnp.float32)
            inward_part[m] = total.astype(jnp.bfloat16)

            @pl.when(depth < middle)
            def _():
                inward_copy(m, inward_part.at[m]).start()

            @pl.when(depth == middle)
            def _():
                cross_copy(m).start()

    def send_outward(m):
        @pl.when(depth == middle)
        def _():
            cross_copy(m).wait_recv()
            total = inward_part[m].astype(jnp.float32) + cross_part[m].astype(jnp.float32)
            place(gathered, m)[...] = total.astype(jnp.bfloat16)
            outward_copy(m).start()
            squares[0, pl.ds(lax.div(m, per_layer), 1), :] += jnp.sum(total * total, axis=0, keepdims=True)

        @pl.when(depth < middle)
        def _():
            outward_copy(m).wait_recv()

            @pl.when(depth > 0)
            def _():
                outward_copy(m).start()

        @pl.when(lax.rem(m, GROUP) == GROUP - 1)
        def _():
            k = lax.div(m, per_layer)
            first = pl.multiple_of((lax.rem(m, per_layer) - (GROUP - 1)) * TILE, TILE)
            band = gathered[k, :, pl.ds(first, GROUP * TILE)]
            gram[k] += lax.dot_general(band, band, (((1,), (1,)), ((), ())), preferred_element_type=jnp.float32)

    wait_for = (2 * middle + 1 - 2 * depth) * LAG

    def step(t, carry):
        @pl.when(t < messages)
        def _():
            send_inward(t)

        @pl.when(t >= wait_for)
        def _():
            send_outward(t - wait_for)

        return carry

    lax.fori_loop(0, messages + wait_for, step, 0)

    def plane_copies():
        return [
            pltpu.make_async_remote_copy(
                src_ref=squares.at[0], dst_ref=plane_in.at[at], send_sem=plane_send.at[at],
                recv_sem=plane_recv.at[at], device_id=across(*offset), device_id_type=MESH)
            for at, offset in enumerate(offsets)
        ]

    reach = ring // 2

    def ring_copy(offset):
        return pltpu.make_async_remote_copy(
            src_ref=squares.at[1], dst_ref=ring_in.at[half], send_sem=ring_send.at[offset],
            recv_sem=ring_recv.at[half], device_id=along_z(lax.rem(ring + (2 * upper - 1) * offset, ring)),
            device_id_type=MESH)

    def ring_arrival(source):
        return pltpu.make_async_remote_copy(
            src_ref=squares.at[1], dst_ref=ring_in.at[source], send_sem=ring_send.at[0],
            recv_sem=ring_recv.at[source], device_id=up, device_id_type=MESH)

    @pl.when(depth == middle)
    def _():
        copies = plane_copies()
        for copy in copies:
            copy.start()
        total = squares[0]
        for at, copy in enumerate(copies):
            copy.wait_recv()
            total = total + plane_in[at]
        squares[1] = total
        for offset in range(1, reach):
            ring_copy(offset).start()

    for k in range(layers):
        average = (gathered[k, :, mine].astype(jnp.float32) - mixed * moment[k]) / n
        fresh[k] = MOMENTUM_RATE * moment[k] + average
    pltpu.make_async_copy(fresh, next_hbm, store_sem.at[0]).start()

    for source in range(halves):
        @pl.when((depth == middle) & (half == source))
        def _():
            ring_in[source] = squares[1]

        @pl.when((depth != middle) | (half != source))
        def _():
            ring_arrival(source).wait_recv()

    total = ring_in[0]
    for source in range(1, halves):
        total = total + ring_in[source]

    eye = (lax.broadcasted_iota(jnp.int32, (rows, rows), 0) == lax.broadcasted_iota(jnp.int32, (rows, rows), 1))
    eye = eye.astype(jnp.float32)
    product = functools.partial(jnp.dot, precision=EXACTNESS, preferred_element_type=jnp.float32)
    factors, states, mixes = [], [], []
    for k in range(layers):
        norm = gain * jnp.sqrt(jnp.sum(total[k : k + 1, :], axis=1, keepdims=True))
        factor = gain / (norm + EPSILON)
        factors.append(factor)
        states.append(gram[k] * (factor * factor))
        mixes.append(None)
    for iteration in range(ITERS):
        for k in range(layers):
            state = states[k]
            square = product(state, state)
            poly = QUINTIC_FIRST * eye + QUINTIC_SECOND * state + QUINTIC_THIRD * square
            mixes[k] = poly if mixes[k] is None else product(poly, mixes[k])
            if iteration + 1 < ITERS:
                states[k] = product(product(state, poly), poly)

    span = cols // 4
    for k in range(layers):
        mix = mixes[k] * (factors[k] * math.sqrt(cols))
        high = mix.astype(jnp.bfloat16)
        low = (mix - high.astype(jnp.float32)).astype(jnp.bfloat16)
        for at in range(cols // span):
            window = pl.ds(at * span, span)
            block = gathered[k, :, window]
            value = jnp.dot(high, block, preferred_element_type=jnp.float32)
            value = value + jnp.dot(low, block, preferred_element_type=jnp.float32)
            result[k, :, window] = value.astype(jnp.bfloat16)
            pltpu.make_async_copy(
                result.at[k, :, window], out_hbm.at[k, :, window], store_sem.at[1 + k * (cols // span) + at]).start()

    def drain(m, carry):
        inward_copy(m, inward_part.at[m]).wait_send()

        @pl.when(depth > 0)
        def _():
            outward_copy(m).wait_send()

        return carry

    lax.fori_loop(0, messages, drain, 0)

    @pl.when(depth == middle)
    def _():
        for copy in plane_copies():
            copy.wait_send()
        for offset in range(1, reach):
            ring_copy(offset).wait_send()

    pltpu.make_async_copy(fresh, next_hbm, store_sem.at[0]).wait()
    for k in range(layers):
        for at in range(cols // span):
            window = pl.ds(at * span, span)
            pltpu.make_async_copy(
                result.at[k, :, window], out_hbm.at[k, :, window], store_sem.at[1 + k * (cols // span) + at]).wait()


def body(axes, pseudo_grads, momentum):
    n = lax.axis_size("replica")
    _, layers, rows, cols = pseudo_grads.shape
    width = cols // n
    messages = layers * cols // TILE
    ring = axes[0] * n
    plane = max(axes[1] * axes[2] * axes[3] - 1, 1)
    dma = pltpu.SemaphoreType.DMA
    any_spec = pl.BlockSpec(memory_space=pl.ANY)
    bf16, f32 = jnp.bfloat16, jnp.float32
    return pl.pallas_call(
        functools.partial(kernel, n, axes),
        out_shape=(
            jax.ShapeDtypeStruct((layers, rows, cols), bf16),
            jax.ShapeDtypeStruct((layers, rows, width), f32),
        ),
        in_specs=[any_spec, any_spec],
        out_specs=(any_spec, any_spec),
        scratch_shapes=[
            pltpu.VMEM((layers, rows, cols), bf16),
            pltpu.VMEM((layers, rows, width), f32),
            pltpu.VMEM((layers, rows, width), f32),
            pltpu.VMEM((layers, rows, cols), bf16),
            pltpu.VMEM((messages, rows, TILE), bf16),
            pltpu.VMEM((messages, rows, TILE), bf16),
            pltpu.VMEM((layers, rows, rows), f32),
            pltpu.VMEM((2, 8, TILE), f32),
            pltpu.VMEM((plane, 8, TILE), f32),
            pltpu.VMEM((axes[0], 8, TILE), f32),
            pltpu.VMEM((layers, rows, cols), bf16),
            dma((2,)),
            dma((messages,)),
            dma((messages,)),
            dma((messages,)),
            dma((messages,)),
            dma((messages,)),
            dma((plane,)),
            dma((plane,)),
            dma((ring,)),
            dma((axes[0],)),
            dma((16,)),
        ],
        compiler_params=pltpu.CompilerParams(
            collective_id=0, has_side_effects=True, vmem_limit_bytes=40 * 1024 * 1024),
    )(pseudo_grads, momentum)


def solution(mesh, axes=SHARD_AXES):
    placed = (P("replica", None, "shard", None), P(None, "shard", "replica"))
    return jax.shard_map(
        functools.partial(body, axes),
        mesh=mesh,
        in_specs=placed,
        out_specs=(P(None, "shard", None), P(None, "shard", "replica")),
        check_vma=False,
    )
```

```python
import functools
import math

import jax
import jax.numpy as jnp
from jax import lax
from jax.experimental import pallas as pl
from jax.experimental.pallas import tpu as pltpu
from jax.sharding import PartitionSpec as P

ITERS = 5
QUINTIC_FIRST = 3.4445
QUINTIC_SECOND = -4.775
QUINTIC_THIRD = 2.0315
MOMENTUM_RATE = 0.9
EPSILON = 1e-07
EXACTNESS = lax.Precision.HIGHEST
MESH = pl.DeviceIdType.MESH

SHARD_AXES = (2, 4, 4, 2)
TILE = 128
EARLY = 8
PIECES = 4
GROUP = 8
LAG = 9


def rates(n):
    gain = (1.0 + MOMENTUM_RATE) / n
    return gain, MOMENTUM_RATE * MOMENTUM_RATE / gain


def kernel(
    n, axes, grads_hbm, moment_hbm, gathered, mix_out,
    grads, moment, inward_part, cross_part, gram, squares, plane_in, ring_in,
    load_sem, inward_recv, cross_recv, outward_recv, inward_send, outward_send,
    plane_send, plane_recv, ring_send, ring_recv,
):
    halves, xs, ys, cores = axes
    layers, rows, cols = grads.shape
    width = cols // n
    per_layer = cols // TILE
    messages = layers * per_layer
    ring = halves * n
    middle = n // 2 - 1

    gain, mixed = rates(n)

    i = lax.axis_index("replica")
    shard = lax.axis_index("shard")
    half = lax.div(shard, cores * ys * xs)
    z = half * n + i
    in_plane = shard - half * (cores * ys * xs)
    upper = lax.div(i, n // 2)
    depth = i + upper * (n - 1 - 2 * i)
    inward = (i + 1 - 2 * upper, shard)
    outward = (i - 1 + 2 * upper, shard)

    def along_z(offset):
        there = lax.rem(z + offset, ring)
        return (lax.rem(there, n), lax.div(there, n) * (cores * ys * xs) + in_plane)

    plane = xs * ys * cores
    offsets = range(1, plane)

    def across(offset):
        return (i, half * plane + lax.rem(in_plane + offset, plane))

    loads = [
        pltpu.make_async_copy(moment_hbm, moment, load_sem.at[0]),
        pltpu.make_async_copy(grads_hbm.at[0], grads, load_sem.at[1]),
    ]
    for load in loads:
        load.start()

    barrier = pltpu.get_barrier_semaphore()
    pl.semaphore_signal(barrier, inc=1, device_id=inward, device_id_type=MESH)

    @pl.when(depth > 0)
    def _():
        pl.semaphore_signal(barrier, inc=1, device_id=outward, device_id_type=MESH)

    if halves > 1:
        far = (n // 2 - upper, lax.rem(half + 1, halves) * (cores * ys * xs) + in_plane)
        pl.semaphore_signal(barrier, inc=1, device_id=far, device_id_type=MESH)

    @pl.when(depth == middle)
    def _():
        for offset in offsets:
            pl.semaphore_signal(barrier, inc=1, device_id=across(offset), device_id_type=MESH)

    def place(ref, m):
        column = pl.multiple_of(lax.rem(lax.rem(m, per_layer) + EARLY, per_layer) * TILE, TILE)
        return ref.at[lax.div(m, per_layer), :, pl.ds(column, TILE)]

    def inward_copy(m, source):
        return pltpu.make_async_remote_copy(
            src_ref=source, dst_ref=inward_part.at[m], send_sem=inward_send, recv_sem=inward_recv.at[m],
            device_id=inward, device_id_type=MESH)

    def cross_copy(m):
        return pltpu.make_async_remote_copy(
            src_ref=inward_part.at[m], dst_ref=cross_part.at[m], send_sem=inward_send,
            recv_sem=cross_recv.at[m], device_id=inward, device_id_type=MESH)

    def outward_copy(m):
        chunk = place(gathered, m)
        return pltpu.make_async_remote_copy(
            src_ref=chunk, dst_ref=chunk, send_sem=outward_send, recv_sem=outward_recv.at[m],
            device_id=outward, device_id_type=MESH)

    def send_inward(m):
        own = place(grads, m)

        @pl.when((depth == 0) & (m >= EARLY))
        def _():
            inward_copy(m, own).start()

        @pl.when(depth > 0)
        def _():
            inward_copy(m, own).wait_recv()
            total = inward_part[m].astype(jnp.float32) + own[...].astype(jnp.float32)
            inward_part[m] = total.astype(jnp.bfloat16)

            @pl.when(depth < middle)
            def _():
                inward_copy(m, inward_part.at[m]).start()

            @pl.when(depth == middle)
            def _():
                cross_copy(m).start()

    def send_outward(m):
        @pl.when(depth == middle)
        def _():
            cross_copy(m).wait_recv()
            total = inward_part[m].astype(jnp.float32) + cross_part[m].astype(jnp.float32)
            place(gathered, m)[...] = total.astype(jnp.bfloat16)
            outward_copy(m).start()
            squares[0, pl.ds(lax.div(m, per_layer), 1), :] += jnp.sum(total * total, axis=0, keepdims=True)

        @pl.when(depth < middle)
        def _():
            outward_copy(m).wait_recv()

            @pl.when(depth > 0)
            def _():
                outward_copy(m).start()

        @pl.when(lax.rem(m, GROUP) == GROUP - 1)
        def _():
            k = lax.div(m, per_layer)
            first = lax.rem(lax.rem(m, per_layer) - (GROUP - 1) + EARLY, per_layer)
            first = pl.multiple_of(first * TILE, TILE)
            band = gathered[k, :, pl.ds(first, GROUP * TILE)]
            gram[k] += lax.dot_general(band, band, (((1,), (1,)), ((), ())), preferred_element_type=jnp.float32)

    gram[...] = jnp.zeros_like(gram)
    squares[...] = jnp.zeros_like(squares)

    @pl.when(depth == 0)
    def _():
        pl.semaphore_wait(barrier, 1)
        for m in range(EARLY):
            inward_copy(m, place(grads_hbm.at[0], m)).start()

    for load in loads:
        load.wait()
    mine = pl.ds(pl.multiple_of(i * width, TILE), width)
    for k in range(layers):
        own = grads[k, :, mine].astype(jnp.float32) + mixed * moment[k]
        grads[k, :, mine] = own.astype(jnp.bfloat16)

    @pl.when((depth > 0) & (depth < middle))
    def _():
        pl.semaphore_wait(barrier, 2)

    @pl.when(depth == middle)
    def _():
        pl.semaphore_wait(barrier, 2 + len(offsets) + (halves - 1) * (n // 2))

    wait_for = (2 * middle + 1 - 2 * depth) * LAG

    def step(t, carry):
        @pl.when(t < messages)
        def _():
            send_inward(t)

        @pl.when(t >= wait_for)
        def _():
            send_outward(t - wait_for)

        return carry

    lax.fori_loop(0, messages + wait_for, step, 0)

    def plane_copies():
        return [
            pltpu.make_async_remote_copy(
                src_ref=squares.at[0], dst_ref=plane_in.at[at], send_sem=plane_send.at[at],
                recv_sem=plane_recv.at[at], device_id=across(offset), device_id_type=MESH)
            for at, offset in enumerate(offsets)
        ]

    reach = ring // 2

    def ring_copy(offset):
        return pltpu.make_async_remote_copy(
            src_ref=squares.at[1], dst_ref=ring_in.at[half], send_sem=ring_send.at[offset],
            recv_sem=ring_recv.at[half], device_id=along_z(lax.rem(ring + (2 * upper - 1) * offset, ring)),
            device_id_type=MESH)

    def ring_arrival(source):
        return pltpu.make_async_remote_copy(
            src_ref=squares.at[1], dst_ref=ring_in.at[source], send_sem=ring_send.at[0],
            recv_sem=ring_recv.at[source], device_id=inward, device_id_type=MESH)

    @pl.when(depth == middle)
    def _():
        copies = plane_copies()
        for copy in copies:
            copy.start()
        total = squares[0]
        for at, copy in enumerate(copies):
            copy.wait_recv()
            total = total + plane_in[at]
        squares[1] = total
        for offset in range(1, reach):
            ring_copy(offset).start()

    pltpu.make_async_copy(grads, grads, inward_send).wait()

    @pl.when(depth > 0)
    def _():
        pltpu.make_async_copy(grads, grads, outward_send).wait()

    for source in range(halves):
        @pl.when((depth == middle) & (half == source))
        def _():
            ring_in[source] = squares[1]

        @pl.when((depth != middle) | (half != source))
        def _():
            ring_arrival(source).wait_recv()

    total = ring_in[0]
    for source in range(1, halves):
        total = total + ring_in[source]

    eye = (lax.broadcasted_iota(jnp.int32, (rows, rows), 0) == lax.broadcasted_iota(jnp.int32, (rows, rows), 1))
    eye = eye.astype(jnp.float32)
    product = functools.partial(jnp.dot, precision=EXACTNESS, preferred_element_type=jnp.float32)
    factors, states, mixes = [], [], []
    for k in range(layers):
        norm = gain * jnp.sqrt(jnp.sum(total[k : k + 1, :], axis=1, keepdims=True))
        factor = gain / (norm + EPSILON)
        factors.append(factor)
        states.append(gram[k] * (factor * factor))
        mixes.append(None)
    for iteration in range(ITERS):
        for k in range(layers):
            state = states[k]
            square = product(state, state)
            poly = QUINTIC_FIRST * eye + QUINTIC_SECOND * state + QUINTIC_THIRD * square
            mixes[k] = poly if mixes[k] is None else product(poly, mixes[k])
            if iteration + 1 < ITERS:
                states[k] = product(product(state, poly), poly)

    for k in range(layers):
        mix_out[k] = mixes[k] * (factors[k] * math.sqrt(cols))

    @pl.when(depth == middle)
    def _():
        for copy in plane_copies():
            copy.wait_send()
        for offset in range(1, reach):
            ring_copy(offset).wait_send()


def finish(n, gathered, mix, moment_hbm, out_hbm, next_hbm, moment, fresh, result, load_sem, store_sem):
    layers, rows, cols = gathered.shape
    width = cols // n
    mixed = rates(n)[1]
    load = pltpu.make_async_copy(moment_hbm, moment, load_sem)
    load.start()
    span = cols // PIECES
    stores = []
    for k in range(layers):
        high = mix[k].astype(jnp.bfloat16)
        low = (mix[k] - high.astype(jnp.float32)).astype(jnp.bfloat16)
        both = jnp.concatenate([high, low], axis=0)
        for at in range(PIECES):
            window = pl.ds(at * span, span)
            value = jnp.dot(both, gathered[k, :, window], preferred_element_type=jnp.float32)
            result[k, :, window] = (value[:rows] + value[rows:]).astype(jnp.bfloat16)
            stores.append(pltpu.make_async_copy(
                result.at[k, :, window], out_hbm.at[k, :, window], store_sem.at[1 + k * PIECES + at]))
            stores[-1].start()
        if k == 0:
            load.wait()
            mine = pl.ds(pl.multiple_of(lax.axis_index("replica") * width, TILE), width)
            for every in range(layers):
                average = (gathered[every, :, mine].astype(jnp.float32) - mixed * moment[every]) / n
                fresh[every] = MOMENTUM_RATE * moment[every] + average
            stores.append(pltpu.make_async_copy(fresh, next_hbm, store_sem.at[0]))
            stores[-1].start()
    for store in stores:
        store.wait()


def body(axes, pseudo_grads, momentum):
    n = lax.axis_size("replica")
    _, layers, rows, cols = pseudo_grads.shape
    width = cols // n
    messages = layers * cols // TILE
    ring = axes[0] * n
    plane = max(axes[1] * axes[2] * axes[3] - 1, 1)
    dma = pltpu.SemaphoreType.DMA
    any_spec = pl.BlockSpec(memory_space=pl.ANY)
    vmem_spec = pl.BlockSpec(memory_space=pltpu.VMEM)
    bf16, f32 = jnp.bfloat16, jnp.float32
    momentum = pltpu.with_memory_space_constraint(momentum, pltpu.HBM)
    gathered, mix = pl.pallas_call(
        functools.partial(kernel, n, axes),
        out_shape=(
            jax.ShapeDtypeStruct((layers, rows, cols), bf16),
            jax.ShapeDtypeStruct((layers, rows, rows), f32),
        ),
        in_specs=[any_spec, any_spec],
        out_specs=(vmem_spec, vmem_spec),
        scratch_shapes=[
            pltpu.VMEM((layers, rows, cols), bf16),
            pltpu.VMEM((layers, rows, width), f32),
            pltpu.VMEM((messages, rows, TILE), bf16),
            pltpu.VMEM((messages, rows, TILE), bf16),
            pltpu.VMEM((layers, rows, rows), f32),
            pltpu.VMEM((2, 2, TILE), f32),
            pltpu.VMEM((plane, 2, TILE), f32),
            pltpu.VMEM((axes[0], 2, TILE), f32),
            dma((2,)),
            dma((messages,)),
            dma((messages,)),
            dma((messages,)),
            dma,
            dma,
            dma((plane,)),
            dma((plane,)),
            dma((ring,)),
            dma((axes[0],)),
        ],
        compiler_params=pltpu.CompilerParams(
            collective_id=0, has_side_effects=True, vmem_limit_bytes=40 * 1024 * 1024),
    )(pltpu.with_memory_space_constraint(pseudo_grads, pltpu.HBM), momentum)
    return pl.pallas_call(
        functools.partial(finish, n),
        out_shape=(
            jax.ShapeDtypeStruct((layers, rows, cols), bf16),
            jax.ShapeDtypeStruct((layers, rows, width), f32),
        ),
        in_specs=[vmem_spec, vmem_spec, any_spec],
        out_specs=(any_spec, any_spec),
        scratch_shapes=[
            pltpu.VMEM((layers, rows, width), f32),
            pltpu.VMEM((layers, rows, width), f32),
            pltpu.VMEM((layers, rows, cols), bf16),
            dma,
            dma((1 + layers * PIECES,)),
        ],
        compiler_params=pltpu.CompilerParams(vmem_limit_bytes=40 * 1024 * 1024),
    )(gathered, mix, momentum)


def solution(mesh, axes=SHARD_AXES):
    placed = (P("replica", None, "shard", None), P(None, "shard", "replica"))
    return jax.shard_map(
        functools.partial(body, axes),
        mesh=mesh,
        in_specs=placed,
        out_specs=(P(None, "shard", None), P(None, "shard", "replica")),
        check_vma=False,
    )
```

```python
import functools
import math

import jax
import jax.numpy as jnp
from jax import lax
from jax.experimental import pallas as pl
from jax.experimental.pallas import tpu as pltpu
from jax.sharding import PartitionSpec as P

ITERS = 5
QUINTIC_FIRST = 3.4445
QUINTIC_SECOND = -4.775
QUINTIC_THIRD = 2.0315
MOMENTUM_RATE = 0.9
EPSILON = 1e-07
TINY = 1e-30
EXACTNESS = lax.Precision.HIGHEST
MESH = pl.DeviceIdType.MESH

SHARD_AXES = (2, 4, 4, 2)
LANES = 128
TILE = 256
EARLY = 4
PIECES = 4
GROUP = 4
LAG_MIDDLE = 5
BURST = 4
SETTLE = 14
LAG = 5


def rates(n):
    gain = (1.0 + MOMENTUM_RATE) / n
    return gain, MOMENTUM_RATE * MOMENTUM_RATE / gain


def kernel(
    n, axes, grads_hbm, moment_hbm, gathered, mix_out, done_out,
    grads, moment, inward_part, cross_part, gram, squares, plane_in, ring_in,
    load_sem, inward_recv, cross_recv, outward_recv, inward_send, outward_send,
    plane_send, plane_recv, ring_send, ring_recv,
):
    halves, xs, ys, cores = axes
    layers, rows, cols = grads.shape
    width = cols // n
    per_layer = cols // TILE
    messages = layers * per_layer
    ring = halves * n
    middle = n // 2 - 1

    gain, mixed = rates(n)

    i = lax.axis_index("replica")
    shard = lax.axis_index("shard")
    half = lax.div(shard, cores * ys * xs)
    z = half * n + i
    in_plane = shard - half * (cores * ys * xs)
    upper = lax.div(i, n // 2)
    depth = i + upper * (n - 1 - 2 * i)
    inward = (i + 1 - 2 * upper, shard)
    outward = (i - 1 + 2 * upper, shard)

    def along_z(offset):
        there = lax.rem(z + offset, ring)
        return (lax.rem(there, n), lax.div(there, n) * (cores * ys * xs) + in_plane)

    plane = xs * ys * cores
    offsets = range(1, plane)

    def across(offset):
        return (i, half * plane + lax.rem(in_plane + offset, plane))

    loads = [
        pltpu.make_async_copy(moment_hbm, moment, load_sem.at[0]),
        pltpu.make_async_copy(grads_hbm.at[0], grads, load_sem.at[1]),
    ]
    for load in loads:
        load.start()

    barrier = pltpu.get_barrier_semaphore()
    pl.semaphore_signal(barrier, inc=1, device_id=inward, device_id_type=MESH)

    @pl.when(depth > 0)
    def _():
        pl.semaphore_signal(barrier, inc=1, device_id=outward, device_id_type=MESH)

    if halves > 1:
        far = (n // 2 - upper, lax.rem(half + 1, halves) * (cores * ys * xs) + in_plane)
        pl.semaphore_signal(barrier, inc=1, device_id=far, device_id_type=MESH)

    @pl.when(depth == middle)
    def _():
        for offset in offsets:
            pl.semaphore_signal(barrier, inc=1, device_id=across(offset), device_id_type=MESH)

    def place(ref, m):
        column = pl.multiple_of(lax.rem(lax.rem(m, per_layer) + EARLY, per_layer) * TILE, TILE)
        return ref.at[lax.div(m, per_layer), :, pl.ds(column, TILE)]

    def inward_copy(m, source):
        return pltpu.make_async_remote_copy(
            src_ref=source, dst_ref=inward_part.at[m], send_sem=inward_send, recv_sem=inward_recv.at[m],
            device_id=inward, device_id_type=MESH)

    def cross_copy(m):
        return pltpu.make_async_remote_copy(
            src_ref=inward_part.at[m], dst_ref=cross_part.at[m], send_sem=inward_send,
            recv_sem=cross_recv.at[m], device_id=inward, device_id_type=MESH)

    def outward_copy(m):
        chunk = place(gathered, m)
        return pltpu.make_async_remote_copy(
            src_ref=chunk, dst_ref=chunk, send_sem=outward_send, recv_sem=outward_recv.at[m],
            device_id=outward, device_id_type=MESH)

    def send_inward(m):
        own = place(grads, m)

        @pl.when((depth == 0) & (m >= EARLY))
        def _():
            inward_copy(m, own).start()

        @pl.when(depth > 0)
        def _():
            inward_copy(m, own).wait_recv()
            total = inward_part[m].astype(jnp.float32) + own[...].astype(jnp.float32)
            inward_part[m] = total.astype(jnp.bfloat16)

            @pl.when(depth < middle)
            def _():
                inward_copy(m, inward_part.at[m]).start()

            @pl.when(depth == middle)
            def _():
                cross_copy(m).start()

    def send_outward(m):
        @pl.when(depth == middle)
        def _():
            cross_copy(m).wait_recv()
            total = inward_part[m].astype(jnp.float32) + cross_part[m].astype(jnp.float32)
            place(gathered, m)[...] = total.astype(jnp.bfloat16)
            outward_copy(m).start()
            squares[0, lax.div(m, per_layer)] += jnp.sum(total * total, axis=0, keepdims=True)

        @pl.when(depth < middle)
        def _():
            outward_copy(m).wait_recv()

            @pl.when(depth > 0)
            def _():
                outward_copy(m).start()

        @pl.when(lax.rem(m, GROUP) == GROUP - 1)
        def _():
            k = lax.div(m, per_layer)
            first = lax.rem(lax.rem(m, per_layer) - (GROUP - 1) + EARLY, per_layer)
            first = pl.multiple_of(first * TILE, TILE)
            band = gathered[k, :, pl.ds(first, GROUP * TILE)]
            gram[k] += lax.dot_general(band, band, (((1,), (1,)), ((), ())), preferred_element_type=jnp.float32)

    gram[...] = jnp.zeros_like(gram)
    squares[...] = jnp.zeros_like(squares)

    @pl.when(depth == 0)
    def _():
        pl.semaphore_wait(barrier, 1)
        for m in range(EARLY):
            inward_copy(m, place(grads_hbm.at[0], m)).start()

    for load in loads:
        load.wait()
    mine = pl.ds(pl.multiple_of(i * width, LANES), width)
    for k in range(layers):
        own = grads[k, :, mine].astype(jnp.float32) + mixed * moment[k]
        grads[k, :, mine] = own.astype(jnp.bfloat16)

    @pl.when((depth > 0) & (depth < middle))
    def _():
        pl.semaphore_wait(barrier, 2)

    @pl.when(depth == middle)
    def _():
        pl.semaphore_wait(barrier, 2 + len(offsets) + (halves - 1) * (n // 2))

    wait_for = (2 * middle + 1 - 2 * depth) * LAG - lax.div(depth, middle) * (LAG - LAG_MIDDLE)

    def plane_copy(k, offset):
        return pltpu.make_async_remote_copy(
            src_ref=squares.at[0, k], dst_ref=plane_in.at[k, offset - 1], send_sem=plane_send.at[k],
            recv_sem=plane_recv.at[k], device_id=across(offset), device_id_type=MESH)

    reach = ring // 2

    def ring_copy(k, offset):
        return pltpu.make_async_remote_copy(
            src_ref=squares.at[1, k], dst_ref=ring_in.at[k, half], send_sem=ring_send.at[k, offset],
            recv_sem=ring_recv.at[k, half], device_id=along_z(lax.rem(ring + (2 * upper - 1) * offset, ring)),
            device_id_type=MESH)

    def plane_sum(k):
        if plane > 1:
            pltpu.make_async_copy(plane_in.at[k], plane_in.at[k], plane_recv.at[k]).wait()
        total = squares[0, k]
        for at in range(plane - 1):
            total = total + plane_in[k, at]
        squares[1, k] = total
        for offset in range(1, reach):
            ring_copy(k, offset).start()

    def norm_factor(k):
        total = jnp.zeros((1, TILE), jnp.float32)
        for source in range(halves):
            @pl.when((depth == middle) & (half == source))
            def _():
                ring_in[k, source] = squares[1, k]

            @pl.when((depth != middle) | (half != source))
            def _():
                pltpu.make_async_remote_copy(
                    src_ref=squares.at[1, k], dst_ref=ring_in.at[k, source], send_sem=ring_send.at[k, 0],
                    recv_sem=ring_recv.at[k, source], device_id=inward, device_id_type=MESH).wait_recv()

            total = total + ring_in[k, source]
        norm = gain * jnp.sqrt(jnp.sum(total, axis=1, keepdims=True))
        return gain / (norm + EPSILON)

    def step(t, carry):
        @pl.when(t < messages)
        def _():
            send_inward(t)

        @pl.when(t >= wait_for)
        def _():
            send_outward(t - wait_for)

        for k in range(layers - 1):
            since = t - wait_for - (k + 1) * per_layer

            for q in range(BURST):
                @pl.when((depth == middle) & (since >= 0) & (since * BURST + q + 1 < plane))
                def _():
                    plane_copy(k, since * BURST + q + 1).start()

            @pl.when((depth == middle) & (since == SETTLE))
            def _():
                plane_sum(k)

        return carry

    lax.fori_loop(0, messages + wait_for, step, 0)

    eye = (lax.broadcasted_iota(jnp.int32, (rows, rows), 0) == lax.broadcasted_iota(jnp.int32, (rows, rows), 1))
    eye = eye.astype(jnp.float32)
    product = functools.partial(jnp.dot, precision=EXACTNESS, preferred_element_type=jnp.float32)

    def polynomial(state, square):
        return QUINTIC_FIRST * eye + QUINTIC_SECOND * state + QUINTIC_THIRD * square

    def newton_schulz(state, mix, count):
        for iteration in range(count):
            poly = polynomial(state, product(state, state))
            mix = poly if mix is None else product(poly, mix)
            if iteration + 1 < count:
                state = product(product(state, poly), poly)
        return mix

    final = layers - 1

    @pl.when(depth == middle)
    def _():
        for offset in offsets:
            plane_copy(final, offset).start()

    early = []
    for k in range(final):
        factor = norm_factor(k)
        early.append(newton_schulz(gram[k] * (factor * factor), None, ITERS) * (factor * math.sqrt(cols)))

    @pl.when(depth == middle)
    def _():
        plane_sum(final)

    for k in range(final):
        apply_mix(early[k], gathered, k, lambda window, value: done_out.__setitem__((k, slice(None), window), value))

    trace = jnp.sum(gram[final] * eye, axis=(0, 1), keepdims=True) + TINY
    one = gram[final] / trace
    two = product(one, one)
    three, four = product(one, two), product(two, two)
    five = product(two, three)
    a, b, c = QUINTIC_FIRST, QUINTIC_SECOND, QUINTIC_THIRD
    factor = norm_factor(final)
    share = factor * factor * trace
    mix = polynomial(share * one, (share * share) * two)
    state = share * (
        a * a * one
        + share * (2.0 * a * b * two
        + share * ((b * b + 2.0 * a * c) * three
        + share * (2.0 * b * c * four
        + share * (c * c * five)))))
    mix = newton_schulz(state, mix, ITERS - 1)
    mix_out[...] = mix * (factor * math.sqrt(cols))

    pltpu.make_async_copy(grads, grads, inward_send).wait()

    @pl.when(depth > 0)
    def _():
        pltpu.make_async_copy(grads, grads, outward_send).wait()

    @pl.when(depth == middle)
    def _():
        for k in range(layers):
            if plane > 1:
                pltpu.make_async_copy(plane_in.at[k], plane_in.at[k], plane_send.at[k]).wait()
            for offset in range(1, reach):
                ring_copy(k, offset).wait_send()


def apply_mix(mix, gathered, k, put):
    rows, cols = gathered.shape[1:]
    high = mix.astype(jnp.bfloat16)
    low = (mix - high.astype(jnp.float32)).astype(jnp.bfloat16)
    both = jnp.concatenate([high, low], axis=0)
    span = cols // PIECES
    for at in range(PIECES):
        window = pl.ds(at * span, span)
        value = jnp.dot(both, gathered[k, :, window], preferred_element_type=jnp.float32)
        put(window, (value[:rows] + value[rows:]).astype(jnp.bfloat16))


def finish(n, gathered, mix, done, moment_hbm, out_hbm, next_hbm, moment, fresh, result, load_sem, store_sem):
    layers, rows, cols = gathered.shape
    width = cols // n
    final = layers - 1
    mixed = rates(n)[1]
    load = pltpu.make_async_copy(moment_hbm, moment, load_sem)
    load.start()
    stores = [pltpu.make_async_copy(done, out_hbm.at[pl.ds(0, final)], store_sem.at[0])]
    stores[-1].start()

    def put(window, value):
        result[:, window] = value
        store = pltpu.make_async_copy(
            result.at[:, window], out_hbm.at[final, :, window], store_sem.at[len(stores)])
        store.start()
        stores.append(store)

    apply_mix(mix[...], gathered, final, put)
    load.wait()
    mine = pl.ds(pl.multiple_of(lax.axis_index("replica") * width, LANES), width)
    for k in range(layers):
        average = (gathered[k, :, mine].astype(jnp.float32) - mixed * moment[k]) / n
        fresh[k] = MOMENTUM_RATE * moment[k] + average
        stores.append(pltpu.make_async_copy(fresh.at[k], next_hbm.at[k], store_sem.at[len(stores)]))
        stores[-1].start()
    for store in stores:
        store.wait()


def body(axes, pseudo_grads, momentum):
    n = lax.axis_size("replica")
    _, layers, rows, cols = pseudo_grads.shape
    width = cols // n
    messages = layers * cols // TILE
    ring = axes[0] * n
    plane = max(axes[1] * axes[2] * axes[3] - 1, 1)
    dma = pltpu.SemaphoreType.DMA
    any_spec = pl.BlockSpec(memory_space=pl.ANY)
    vmem_spec = pl.BlockSpec(memory_space=pltpu.VMEM)
    bf16, f32 = jnp.bfloat16, jnp.float32
    momentum = pltpu.with_memory_space_constraint(momentum, pltpu.HBM)
    gathered, mix, done = pl.pallas_call(
        functools.partial(kernel, n, axes),
        out_shape=(
            jax.ShapeDtypeStruct((layers, rows, cols), bf16),
            jax.ShapeDtypeStruct((rows, rows), f32),
            jax.ShapeDtypeStruct((layers - 1, rows, cols), bf16),
        ),
        in_specs=[any_spec, any_spec],
        out_specs=(vmem_spec, vmem_spec, vmem_spec),
        scratch_shapes=[
            pltpu.VMEM((layers, rows, cols), bf16),
            pltpu.VMEM((layers, rows, width), f32),
            pltpu.VMEM((messages, rows, TILE), bf16),
            pltpu.VMEM((messages, rows, TILE), bf16),
            pltpu.VMEM((layers, rows, rows), f32),
            pltpu.VMEM((2, layers, 1, TILE), f32),
            pltpu.VMEM((layers, plane, 1, TILE), f32),
            pltpu.VMEM((layers, axes[0], 1, TILE), f32),
            dma((2,)),
            dma((messages,)),
            dma((messages,)),
            dma((messages,)),
            dma,
            dma,
            dma((layers,)),
            dma((layers,)),
            dma((layers, ring)),
            dma((layers, axes[0])),
        ],
        compiler_params=pltpu.CompilerParams(
            collective_id=0, has_side_effects=True, vmem_limit_bytes=40 * 1024 * 1024),
    )(pltpu.with_memory_space_constraint(pseudo_grads, pltpu.HBM), momentum)
    return pl.pallas_call(
        functools.partial(finish, n),
        out_shape=(
            jax.ShapeDtypeStruct((layers, rows, cols), bf16),
            jax.ShapeDtypeStruct((layers, rows, width), f32),
        ),
        in_specs=[vmem_spec, vmem_spec, vmem_spec, any_spec],
        out_specs=(any_spec, any_spec),
        scratch_shapes=[
            pltpu.VMEM((layers, rows, width), f32),
            pltpu.VMEM((layers, rows, width), f32),
            pltpu.VMEM((rows, cols), bf16),
            dma,
            dma((1 + layers + PIECES,)),
        ],
        compiler_params=pltpu.CompilerParams(vmem_limit_bytes=40 * 1024 * 1024),
    )(gathered, mix, done, momentum)


def solution(mesh, axes=SHARD_AXES):
    placed = (P("replica", None, "shard", None), P(None, "shard", "replica"))
    return jax.shard_map(
        functools.partial(body, axes),
        mesh=mesh,
        in_specs=placed,
        out_specs=(P(None, "shard", None), P(None, "shard", "replica")),
        check_vma=False,
    )
```

```python
import functools
import math

import jax
import jax.numpy as jnp
from jax import lax
from jax.experimental import pallas as pl
from jax.experimental.pallas import tpu as pltpu
from jax.sharding import PartitionSpec as P

ITERS = 5
QUINTIC_FIRST = 3.4445
QUINTIC_SECOND = -4.775
QUINTIC_THIRD = 2.0315
MOMENTUM_RATE = 0.9
EPSILON = 1e-07
TINY = 1e-30
EXACTNESS = lax.Precision.HIGHEST
MESH = pl.DeviceIdType.MESH

SHARD_AXES = (2, 4, 4, 2)
LANES = 128
TILE = 256
EARLY = 4
PIECES = 4
GROUP = 4
BURST = 4
SETTLE = 14
LAGS = (35, 23, 14, 5)


def rates(n):
    gain = (1.0 + MOMENTUM_RATE) / n
    return gain, MOMENTUM_RATE * MOMENTUM_RATE / gain


def kernel(
    n, axes, grads_hbm, moment_hbm, gathered, mix_out, done_out, fresh,
    grads, moment, inward_part, cross_part, gram, squares, plane_in, ring_in,
    load_sem, inward_recv, cross_recv, outward_recv, inward_send, outward_send,
    plane_send, plane_recv, ring_send, ring_recv,
):
    halves, xs, ys, cores = axes
    layers, rows, cols = grads.shape
    width = cols // n
    per_layer = cols // TILE
    messages = layers * per_layer
    ring = halves * n
    middle = n // 2 - 1

    gain, mixed = rates(n)

    i = lax.axis_index("replica")
    shard = lax.axis_index("shard")
    half = lax.div(shard, cores * ys * xs)
    z = half * n + i
    in_plane = shard - half * (cores * ys * xs)
    upper = lax.div(i, n // 2)
    depth = i + upper * (n - 1 - 2 * i)
    inward = (i + 1 - 2 * upper, shard)
    outward = (i - 1 + 2 * upper, shard)

    def along_z(offset):
        there = lax.rem(z + offset, ring)
        return (lax.rem(there, n), lax.div(there, n) * (cores * ys * xs) + in_plane)

    plane = xs * ys * cores
    offsets = range(1, plane)

    def across(offset):
        return (i, half * plane + lax.rem(in_plane + offset, plane))

    loads = [
        pltpu.make_async_copy(moment_hbm, moment, load_sem.at[0]),
        pltpu.make_async_copy(grads_hbm.at[0], grads, load_sem.at[1]),
    ]
    for load in loads:
        load.start()

    barrier = pltpu.get_barrier_semaphore()
    pl.semaphore_signal(barrier, inc=1, device_id=inward, device_id_type=MESH)

    @pl.when(depth > 0)
    def _():
        pl.semaphore_signal(barrier, inc=1, device_id=outward, device_id_type=MESH)

    if halves > 1:
        far = (n // 2 - upper, lax.rem(half + 1, halves) * (cores * ys * xs) + in_plane)
        pl.semaphore_signal(barrier, inc=1, device_id=far, device_id_type=MESH)

    @pl.when(depth == middle)
    def _():
        for offset in offsets:
            pl.semaphore_signal(barrier, inc=1, device_id=across(offset), device_id_type=MESH)

    def place(ref, m):
        column = pl.multiple_of(lax.rem(lax.rem(m, per_layer) + EARLY, per_layer) * TILE, TILE)
        return ref.at[lax.div(m, per_layer), :, pl.ds(column, TILE)]

    def inward_copy(m, source):
        return pltpu.make_async_remote_copy(
            src_ref=source, dst_ref=inward_part.at[m], send_sem=inward_send, recv_sem=inward_recv.at[m],
            device_id=inward, device_id_type=MESH)

    def cross_copy(m):
        return pltpu.make_async_remote_copy(
            src_ref=inward_part.at[m], dst_ref=cross_part.at[m], send_sem=inward_send,
            recv_sem=cross_recv.at[m], device_id=inward, device_id_type=MESH)

    def outward_copy(m):
        chunk = place(gathered, m)
        return pltpu.make_async_remote_copy(
            src_ref=chunk, dst_ref=chunk, send_sem=outward_send, recv_sem=outward_recv.at[m],
            device_id=outward, device_id_type=MESH)

    def send_inward(m):
        own = place(grads, m)

        @pl.when((depth == 0) & (m >= EARLY))
        def _():
            inward_copy(m, own).start()

        @pl.when(depth > 0)
        def _():
            inward_copy(m, own).wait_recv()
            total = inward_part[m].astype(jnp.float32) + own[...].astype(jnp.float32)
            inward_part[m] = total.astype(jnp.bfloat16)

            @pl.when(depth < middle)
            def _():
                inward_copy(m, inward_part.at[m]).start()

            @pl.when(depth == middle)
            def _():
                cross_copy(m).start()

    def send_outward(m):
        @pl.when(depth == middle)
        def _():
            cross_copy(m).wait_recv()
            total = inward_part[m].astype(jnp.float32) + cross_part[m].astype(jnp.float32)
            place(gathered, m)[...] = total.astype(jnp.bfloat16)
            outward_copy(m).start()
            squares[0, lax.div(m, per_layer)] += jnp.sum(total * total, axis=0, keepdims=True)

        @pl.when(depth < middle)
        def _():
            outward_copy(m).wait_recv()

            @pl.when(depth > 0)
            def _():
                outward_copy(m).start()

        @pl.when(lax.rem(m, GROUP) == GROUP - 1)
        def _():
            k = lax.div(m, per_layer)
            first = lax.rem(lax.rem(m, per_layer) - (GROUP - 1) + EARLY, per_layer)
            first = pl.multiple_of(first * TILE, TILE)
            band = gathered[k, :, pl.ds(first, GROUP * TILE)]
            gram[k] += lax.dot_general(band, band, (((1,), (1,)), ((), ())), preferred_element_type=jnp.float32)

    gram[...] = jnp.zeros_like(gram)
    squares[...] = jnp.zeros_like(squares)

    @pl.when(depth == 0)
    def _():
        pl.semaphore_wait(barrier, 1)
        for m in range(EARLY):
            inward_copy(m, place(grads_hbm.at[0], m)).start()

    for load in loads:
        load.wait()
    mine = pl.ds(pl.multiple_of(i * width, LANES), width)
    for k in range(layers):
        own = grads[k, :, mine].astype(jnp.float32) + mixed * moment[k]
        grads[k, :, mine] = own.astype(jnp.bfloat16)

    @pl.when((depth > 0) & (depth < middle))
    def _():
        pl.semaphore_wait(barrier, 2)

    @pl.when(depth == middle)
    def _():
        pl.semaphore_wait(barrier, 2 + len(offsets) + (halves - 1) * (n // 2))

    wait_for = (
        LAGS[0] + lax.div(depth + 2, 3) * (LAGS[1] - LAGS[0]) + lax.div(depth, 2) * (LAGS[2] - LAGS[1])
        + lax.div(depth, 3) * (LAGS[3] - LAGS[2]))

    def plane_copy(k, offset):
        return pltpu.make_async_remote_copy(
            src_ref=squares.at[0, k], dst_ref=plane_in.at[k, offset - 1], send_sem=plane_send.at[k],
            recv_sem=plane_recv.at[k], device_id=across(offset), device_id_type=MESH)

    reach = ring // 2

    def ring_copy(k, offset):
        return pltpu.make_async_remote_copy(
            src_ref=squares.at[1, k], dst_ref=ring_in.at[k, half], send_sem=ring_send.at[k, offset],
            recv_sem=ring_recv.at[k, half], device_id=along_z(lax.rem(ring + (2 * upper - 1) * offset, ring)),
            device_id_type=MESH)

    def plane_sum(k):
        if plane > 1:
            pltpu.make_async_copy(plane_in.at[k], plane_in.at[k], plane_recv.at[k]).wait()
        total = squares[0, k]
        for at in range(plane - 1):
            total = total + plane_in[k, at]
        squares[1, k] = total
        for offset in reversed(range(1, reach)):
            ring_copy(k, offset).start()

    def norm_factor(k):
        total = jnp.zeros((1, TILE), jnp.float32)
        for source in range(halves):
            @pl.when((depth == middle) & (half == source))
            def _():
                ring_in[k, source] = squares[1, k]

            @pl.when((depth != middle) | (half != source))
            def _():
                pltpu.make_async_remote_copy(
                    src_ref=squares.at[1, k], dst_ref=ring_in.at[k, source], send_sem=ring_send.at[k, 0],
                    recv_sem=ring_recv.at[k, source], device_id=inward, device_id_type=MESH).wait_recv()

            total = total + ring_in[k, source]
        norm = gain * jnp.sqrt(jnp.sum(total, axis=1, keepdims=True))
        return gain / (norm + EPSILON)

    def step(t, carry):
        @pl.when(t < messages)
        def _():
            send_inward(t)

        @pl.when(t >= wait_for)
        def _():
            send_outward(t - wait_for)

        for k in range(layers - 1):
            since = t - wait_for - (k + 1) * per_layer

            for q in range(BURST):
                @pl.when((depth == middle) & (since >= 0) & (since * BURST + q + 1 < plane))
                def _():
                    plane_copy(k, since * BURST + q + 1).start()

            @pl.when((depth == middle) & (since == SETTLE))
            def _():
                plane_sum(k)

        return carry

    lax.fori_loop(0, messages + wait_for, step, 0)

    eye = (lax.broadcasted_iota(jnp.int32, (rows, rows), 0) == lax.broadcasted_iota(jnp.int32, (rows, rows), 1))
    eye = eye.astype(jnp.float32)
    product = functools.partial(jnp.dot, precision=EXACTNESS, preferred_element_type=jnp.float32)

    def polynomial(state, square):
        return QUINTIC_FIRST * eye + QUINTIC_SECOND * state + QUINTIC_THIRD * square

    def newton_schulz(state, mix, count):
        for iteration in range(count):
            poly = polynomial(state, product(state, state))
            mix = poly if mix is None else product(poly, mix)
            if iteration + 1 < count:
                state = product(product(state, poly), poly)
        return mix

    final = layers - 1

    @pl.when(depth == middle)
    def _():
        for offset in sorted(offsets, key=lambda o: -links_away(o, axes)):
            plane_copy(final, offset).start()

    early = []
    for k in range(final):
        factor = norm_factor(k)
        early.append(newton_schulz(gram[k] * (factor * factor), None, ITERS) * (factor * math.sqrt(cols)))

    @pl.when(depth == middle)
    def _():
        plane_sum(final)

    for k in range(final):
        apply_mix(early[k], gathered, k, lambda window, value: done_out.__setitem__((k, slice(None), window), value))

    for k in range(layers):
        average = (gathered[k, :, mine].astype(jnp.float32) - mixed * moment[k]) / n
        fresh[k] = MOMENTUM_RATE * moment[k] + average

    trace = jnp.sum(gram[final] * eye, axis=(0, 1), keepdims=True) + TINY
    one = gram[final] / trace
    two = product(one, one)
    three, four = product(one, two), product(two, two)
    five = product(two, three)
    a, b, c = QUINTIC_FIRST, QUINTIC_SECOND, QUINTIC_THIRD
    factor = norm_factor(final)
    share = factor * factor * trace
    mix = polynomial(share * one, (share * share) * two)
    state = share * (
        a * a * one
        + share * (2.0 * a * b * two
        + share * ((b * b + 2.0 * a * c) * three
        + share * (2.0 * b * c * four
        + share * (c * c * five)))))
    mix = newton_schulz(state, mix, ITERS - 1)
    mix_out[...] = mix * (factor * math.sqrt(cols))

    pltpu.make_async_copy(grads, grads, inward_send).wait()

    @pl.when(depth > 0)
    def _():
        pltpu.make_async_copy(grads, grads, outward_send).wait()

    @pl.when(depth == middle)
    def _():
        for k in range(layers):
            if plane > 1:
                pltpu.make_async_copy(plane_in.at[k], plane_in.at[k], plane_send.at[k]).wait()
            for offset in range(1, reach):
                ring_copy(k, offset).wait_send()


def links_away(offset, axes):
    _, xs, ys, cores = axes
    across_x, across_y = offset // (ys * cores), offset // cores % ys
    return min(across_x, xs - across_x) + min(across_y, ys - across_y)


def apply_mix(mix, gathered, k, put):
    rows, cols = gathered.shape[1:]
    high = mix.astype(jnp.bfloat16)
    low = (mix - high.astype(jnp.float32)).astype(jnp.bfloat16)
    both = jnp.concatenate([high, low], axis=0)
    span = cols // PIECES
    for at in range(PIECES):
        window = pl.ds(at * span, span)
        value = jnp.dot(both, gathered[k, :, window], preferred_element_type=jnp.float32)
        put(window, (value[:rows] + value[rows:]).astype(jnp.bfloat16))


def finish(gathered, mix, done, fresh, out_hbm, next_hbm, result, store_sem):
    layers, rows, cols = gathered.shape
    final = layers - 1
    stores = [
        pltpu.make_async_copy(done, out_hbm.at[pl.ds(0, final)], store_sem.at[0]),
        pltpu.make_async_copy(fresh, next_hbm, store_sem.at[1]),
    ]
    for store in stores:
        store.start()

    def put(window, value):
        result[:, window] = value
        store = pltpu.make_async_copy(
            result.at[:, window], out_hbm.at[final, :, window], store_sem.at[len(stores)])
        store.start()
        stores.append(store)

    apply_mix(mix[...], gathered, final, put)
    for store in stores:
        store.wait()


def body(axes, pseudo_grads, momentum):
    n = lax.axis_size("replica")
    _, layers, rows, cols = pseudo_grads.shape
    width = cols // n
    messages = layers * cols // TILE
    ring = axes[0] * n
    plane = max(axes[1] * axes[2] * axes[3] - 1, 1)
    dma = pltpu.SemaphoreType.DMA
    any_spec = pl.BlockSpec(memory_space=pl.ANY)
    vmem_spec = pl.BlockSpec(memory_space=pltpu.VMEM)
    bf16, f32 = jnp.bfloat16, jnp.float32
    gathered, mix, done, fresh = pl.pallas_call(
        functools.partial(kernel, n, axes),
        out_shape=(
            jax.ShapeDtypeStruct((layers, rows, cols), bf16),
            jax.ShapeDtypeStruct((rows, rows), f32),
            jax.ShapeDtypeStruct((layers - 1, rows, cols), bf16),
            jax.ShapeDtypeStruct((layers, rows, width), f32),
        ),
        in_specs=[any_spec, any_spec],
        out_specs=(vmem_spec, vmem_spec, vmem_spec, vmem_spec),
        scratch_shapes=[
            pltpu.VMEM((layers, rows, cols), bf16),
            pltpu.VMEM((layers, rows, width), f32),
            pltpu.VMEM((messages, rows, TILE), bf16),
            pltpu.VMEM((messages, rows, TILE), bf16),
            pltpu.VMEM((layers, rows, rows), f32),
            pltpu.VMEM((2, layers, 1, TILE), f32),
            pltpu.VMEM((layers, plane, 1, TILE), f32),
            pltpu.VMEM((layers, axes[0], 1, TILE), f32),
            dma((2,)),
            dma((messages,)),
            dma((messages,)),
            dma((messages,)),
            dma,
            dma,
            dma((layers,)),
            dma((layers,)),
            dma((layers, ring)),
            dma((layers, axes[0])),
        ],
        compiler_params=pltpu.CompilerParams(
            collective_id=0, has_side_effects=True, vmem_limit_bytes=40 * 1024 * 1024),
    )(pltpu.with_memory_space_constraint(pseudo_grads, pltpu.HBM),
      pltpu.with_memory_space_constraint(momentum, pltpu.HBM))
    return pl.pallas_call(
        finish,
        out_shape=(
            jax.ShapeDtypeStruct((layers, rows, cols), bf16),
            jax.ShapeDtypeStruct((layers, rows, width), f32),
        ),
        in_specs=[vmem_spec, vmem_spec, vmem_spec, vmem_spec],
        out_specs=(any_spec, any_spec),
        scratch_shapes=[
            pltpu.VMEM((rows, cols), bf16),
            dma((2 + PIECES,)),
        ],
        compiler_params=pltpu.CompilerParams(vmem_limit_bytes=40 * 1024 * 1024),
    )(gathered, mix, done, fresh)


def solution(mesh, axes=SHARD_AXES):
    placed = (P("replica", None, "shard", None), P(None, "shard", "replica"))
    return jax.shard_map(
        functools.partial(body, axes),
        mesh=mesh,
        in_specs=placed,
        out_specs=(P(None, "shard", None), P(None, "shard", "replica")),
        check_vma=False,
    )
```

```python
import functools
import math

import jax
import jax.numpy as jnp
from jax import lax
from jax.experimental import pallas as pl
from jax.experimental.pallas import tpu as pltpu
from jax.sharding import PartitionSpec as P

ITERS = 5
QUINTIC_FIRST = 3.4445
QUINTIC_SECOND = -4.775
QUINTIC_THIRD = 2.0315
MOMENTUM_RATE = 0.9
EPSILON = 1e-07
TINY = 1e-30
MESH = pl.DeviceIdType.MESH

SHARD_AXES = (2, 4, 4, 2)
LANES = 128
TILE = 256
EARLY = 4
PIECES = 4
GROUP = 4
BURST = 4
SETTLE = 14
HEADROOM = 6
LAGS = (35, 23, 14, 5)


def rates(n):
    gain = (1.0 + MOMENTUM_RATE) / n
    return gain, MOMENTUM_RATE * MOMENTUM_RATE / gain


def kernel(
    n, axes, grads_hbm, moment_hbm, gathered, mix_out, done_out, fresh,
    grads, moment, inward_part, cross_part, gram, squares, plane_in, ring_in,
    load_sem, inward_recv, cross_recv, outward_recv, inward_send, outward_send,
    plane_send, plane_recv, ring_send, ring_recv,
):
    halves, xs, ys, cores = axes
    layers, rows, cols = grads.shape
    width = cols // n
    per_layer = cols // TILE
    messages = layers * per_layer
    ring = halves * n
    middle = n // 2 - 1

    gain, mixed = rates(n)

    i = lax.axis_index("replica")
    shard = lax.axis_index("shard")
    half = lax.div(shard, cores * ys * xs)
    z = half * n + i
    in_plane = shard - half * (cores * ys * xs)
    upper = lax.div(i, n // 2)
    depth = i + upper * (n - 1 - 2 * i)
    inward = (i + 1 - 2 * upper, shard)
    outward = (i - 1 + 2 * upper, shard)

    def along_z(offset):
        there = lax.rem(z + offset, ring)
        return (lax.rem(there, n), lax.div(there, n) * (cores * ys * xs) + in_plane)

    plane = xs * ys * cores
    offsets = range(1, plane)

    def across(offset):
        return (i, half * plane + lax.rem(in_plane + offset, plane))

    loads = [
        pltpu.make_async_copy(moment_hbm, moment, load_sem.at[0]),
        pltpu.make_async_copy(grads_hbm.at[0], grads, load_sem.at[1]),
    ]
    for load in loads:
        load.start()

    barrier = pltpu.get_barrier_semaphore()
    pl.semaphore_signal(barrier, inc=1, device_id=inward, device_id_type=MESH)

    @pl.when(depth > 0)
    def _():
        pl.semaphore_signal(barrier, inc=1, device_id=outward, device_id_type=MESH)

    if halves > 1:
        far = (n // 2 - upper, lax.rem(half + 1, halves) * (cores * ys * xs) + in_plane)
        pl.semaphore_signal(barrier, inc=1, device_id=far, device_id_type=MESH)

    @pl.when(depth == middle)
    def _():
        for offset in offsets:
            pl.semaphore_signal(barrier, inc=1, device_id=across(offset), device_id_type=MESH)

    def place(ref, m):
        column = pl.multiple_of(lax.rem(lax.rem(m, per_layer) + EARLY, per_layer) * TILE, TILE)
        return ref.at[lax.div(m, per_layer), :, pl.ds(column, TILE)]

    def inward_copy(m, source):
        return pltpu.make_async_remote_copy(
            src_ref=source, dst_ref=inward_part.at[m], send_sem=inward_send, recv_sem=inward_recv.at[m],
            device_id=inward, device_id_type=MESH)

    def cross_copy(m):
        return pltpu.make_async_remote_copy(
            src_ref=inward_part.at[m], dst_ref=cross_part.at[m], send_sem=inward_send,
            recv_sem=cross_recv.at[m], device_id=inward, device_id_type=MESH)

    def outward_copy(m):
        chunk = place(gathered, m)
        return pltpu.make_async_remote_copy(
            src_ref=chunk, dst_ref=chunk, send_sem=outward_send, recv_sem=outward_recv.at[m],
            device_id=outward, device_id_type=MESH)

    def send_inward(m):
        own = place(grads, m)

        @pl.when((depth == 0) & (m >= EARLY))
        def _():
            inward_copy(m, own).start()

        @pl.when(depth > 0)
        def _():
            inward_copy(m, own).wait_recv()
            total = inward_part[m].astype(jnp.float32) + own[...].astype(jnp.float32)
            inward_part[m] = total.astype(jnp.bfloat16)

            @pl.when(depth < middle)
            def _():
                inward_copy(m, inward_part.at[m]).start()

            @pl.when(depth == middle)
            def _():
                cross_copy(m).start()

    def send_outward(m):
        @pl.when(depth == middle)
        def _():
            cross_copy(m).wait_recv()
            total = inward_part[m].astype(jnp.float32) + cross_part[m].astype(jnp.float32)
            place(gathered, m)[...] = total.astype(jnp.bfloat16)
            outward_copy(m).start()
            squares[0, lax.div(m, per_layer)] += jnp.sum(total * total, axis=0, keepdims=True)

        @pl.when(depth < middle)
        def _():
            outward_copy(m).wait_recv()

            @pl.when(depth > 0)
            def _():
                outward_copy(m).start()

        @pl.when(lax.rem(m, GROUP) == GROUP - 1)
        def _():
            k = lax.div(m, per_layer)
            first = lax.rem(lax.rem(m, per_layer) - (GROUP - 1) + EARLY, per_layer)
            first = pl.multiple_of(first * TILE, TILE)
            band = gathered[k, :, pl.ds(first, GROUP * TILE)]
            gram[k] += lax.dot_general(band, band, (((1,), (1,)), ((), ())), preferred_element_type=jnp.float32)

    gram[...] = jnp.zeros_like(gram)
    squares[...] = jnp.zeros_like(squares)

    @pl.when(depth == 0)
    def _():
        pl.semaphore_wait(barrier, 1)
        for m in range(EARLY):
            inward_copy(m, place(grads_hbm.at[0], m)).start()

    for load in loads:
        load.wait()
    mine = pl.ds(pl.multiple_of(i * width, LANES), width)
    for k in range(layers):
        own = grads[k, :, mine].astype(jnp.float32) + mixed * moment[k]
        grads[k, :, mine] = own.astype(jnp.bfloat16)

    @pl.when((depth > 0) & (depth < middle))
    def _():
        pl.semaphore_wait(barrier, 2)

    @pl.when(depth == middle)
    def _():
        pl.semaphore_wait(barrier, 2 + len(offsets) + (halves - 1) * (n // 2))

    wait_for = (
        LAGS[0] + lax.div(depth + 2, 3) * (LAGS[1] - LAGS[0]) + lax.div(depth, 2) * (LAGS[2] - LAGS[1])
        + lax.div(depth, 3) * (LAGS[3] - LAGS[2]))

    def plane_copy(k, offset):
        return pltpu.make_async_remote_copy(
            src_ref=squares.at[0, k], dst_ref=plane_in.at[k, offset - 1], send_sem=plane_send.at[k],
            recv_sem=plane_recv.at[k], device_id=across(offset), device_id_type=MESH)

    reach = ring // 2

    def ring_copy(k, offset):
        return pltpu.make_async_remote_copy(
            src_ref=squares.at[1, k], dst_ref=ring_in.at[k, half], send_sem=ring_send.at[k, offset],
            recv_sem=ring_recv.at[k, half], device_id=along_z(lax.rem(ring + (2 * upper - 1) * offset, ring)),
            device_id_type=MESH)

    def plane_sum(k):
        if plane > 1:
            pltpu.make_async_copy(plane_in.at[k], plane_in.at[k], plane_recv.at[k]).wait()
        total = squares[0, k]
        for at in range(plane - 1):
            total = total + plane_in[k, at]
        squares[1, k] = total
        for offset in reversed(range(1, reach)):
            ring_copy(k, offset).start()

    def norm_factor(k):
        total = jnp.zeros((1, TILE), jnp.float32)
        for source in range(halves):
            @pl.when((depth == middle) & (half == source))
            def _():
                ring_in[k, source] = squares[1, k]

            @pl.when((depth != middle) | (half != source))
            def _():
                pltpu.make_async_remote_copy(
                    src_ref=squares.at[1, k], dst_ref=ring_in.at[k, source], send_sem=ring_send.at[k, 0],
                    recv_sem=ring_recv.at[k, source], device_id=inward, device_id_type=MESH).wait_recv()

            total = total + ring_in[k, source]
        norm = gain * jnp.sqrt(jnp.sum(total, axis=1, keepdims=True))
        return gain / (norm + EPSILON)

    eye = (lax.broadcasted_iota(jnp.int32, (rows, rows), 0) == lax.broadcasted_iota(jnp.int32, (rows, rows), 1))
    eye = eye.astype(jnp.float32)
    def split(value):
        high = value.astype(jnp.bfloat16)
        return high, (value - high.astype(jnp.float32)).astype(jnp.bfloat16)

    def product(a, b):
        dot = functools.partial(jnp.dot, preferred_element_type=jnp.float32)
        (a_high, a_low), (b_high, b_low) = split(a), split(b)
        return dot(a_high, b_high) + (dot(a_high, b_low) + dot(a_low, b_high))


    def polynomial(state, square):
        return QUINTIC_FIRST * eye + QUINTIC_SECOND * state + QUINTIC_THIRD * square

    def newton_schulz(state, mix, count):
        for iteration in range(count):
            poly = polynomial(state, product(state, state))
            mix = poly if mix is None else product(poly, mix)
            if iteration + 1 < count:
                state = product(product(state, poly), poly)
        return mix

    final = layers - 1

    def early_layers():
        for k in range(final):
            factor = norm_factor(k)
            mix = newton_schulz(gram[k] * (factor * factor), None, ITERS) * (factor * math.sqrt(cols))
            apply_mix(mix, gathered, k, lambda window, value: done_out.__setitem__((k, slice(None), window), value))

    steps = messages + wait_for
    early_at = steps - (1 - lax.div(depth + 2, 3)) * HEADROOM

    def step(t, carry):
        @pl.when(t < messages)
        def _():
            send_inward(t)

        @pl.when((t >= wait_for) & (t < steps))
        def _():
            send_outward(t - wait_for)

        for k in range(layers - 1):
            since = t - wait_for - (k + 1) * per_layer

            for q in range(BURST):
                @pl.when((depth == middle) & (since >= 0) & (since * BURST + q + 1 < plane))
                def _():
                    plane_copy(k, since * BURST + q + 1).start()

            @pl.when((depth == middle) & (since == SETTLE))
            def _():
                plane_sum(k)

        @pl.when((depth == middle) & (t == steps))
        def _():
            for offset in sorted(offsets, key=lambda o: -links_away(o, axes)):
                plane_copy(final, offset).start()

        @pl.when(t == early_at)
        def _():
            early_layers()

        return carry

    lax.fori_loop(0, steps + 1, step, 0)

    @pl.when(depth == middle)
    def _():
        plane_sum(final)

    for k in range(layers):
        average = (gathered[k, :, mine].astype(jnp.float32) - mixed * moment[k]) / n
        fresh[k] = MOMENTUM_RATE * moment[k] + average

    trace = jnp.sum(gram[final] * eye, axis=(0, 1), keepdims=True) + TINY
    one = gram[final] / trace
    two = product(one, one)
    three, four = product(one, two), product(two, two)
    five = product(two, three)
    a, b, c = QUINTIC_FIRST, QUINTIC_SECOND, QUINTIC_THIRD
    factor = norm_factor(final)
    share = factor * factor * trace
    mix = polynomial(share * one, (share * share) * two)
    state = share * (
        a * a * one
        + share * (2.0 * a * b * two
        + share * ((b * b + 2.0 * a * c) * three
        + share * (2.0 * b * c * four
        + share * (c * c * five)))))
    mix = newton_schulz(state, mix, ITERS - 1)
    mix_out[...] = mix * (factor * math.sqrt(cols))

    pltpu.make_async_copy(grads, grads, inward_send).wait()

    @pl.when(depth > 0)
    def _():
        pltpu.make_async_copy(grads, grads, outward_send).wait()

    @pl.when(depth == middle)
    def _():
        for k in range(layers):
            if plane > 1:
                pltpu.make_async_copy(plane_in.at[k], plane_in.at[k], plane_send.at[k]).wait()
            for offset in range(1, reach):
                ring_copy(k, offset).wait_send()


def links_away(offset, axes):
    _, xs, ys, cores = axes
    across_x, across_y = offset // (ys * cores), offset // cores % ys
    return min(across_x, xs - across_x) + min(across_y, ys - across_y)


def apply_mix(mix, gathered, k, put):
    rows, cols = gathered.shape[1:]
    high = mix.astype(jnp.bfloat16)
    low = (mix - high.astype(jnp.float32)).astype(jnp.bfloat16)
    both = jnp.concatenate([high, low], axis=0)
    span = cols // PIECES
    for at in range(PIECES):
        window = pl.ds(at * span, span)
        value = jnp.dot(both, gathered[k, :, window], preferred_element_type=jnp.float32)
        put(window, (value[:rows] + value[rows:]).astype(jnp.bfloat16))


def finish(gathered, mix, done, fresh, out_hbm, next_hbm, result, store_sem):
    layers, rows, cols = gathered.shape
    final = layers - 1
    stores = [
        pltpu.make_async_copy(done, out_hbm.at[pl.ds(0, final)], store_sem.at[0]),
        pltpu.make_async_copy(fresh, next_hbm, store_sem.at[1]),
    ]
    for store in stores:
        store.start()

    def put(window, value):
        result[:, window] = value
        store = pltpu.make_async_copy(
            result.at[:, window], out_hbm.at[final, :, window], store_sem.at[len(stores)])
        store.start()
        stores.append(store)

    apply_mix(mix[...], gathered, final, put)
    for store in stores:
        store.wait()


def body(axes, pseudo_grads, momentum):
    n = lax.axis_size("replica")
    _, layers, rows, cols = pseudo_grads.shape
    width = cols // n
    messages = layers * cols // TILE
    ring = axes[0] * n
    plane = max(axes[1] * axes[2] * axes[3] - 1, 1)
    dma = pltpu.SemaphoreType.DMA
    any_spec = pl.BlockSpec(memory_space=pl.ANY)
    vmem_spec = pl.BlockSpec(memory_space=pltpu.VMEM)
    bf16, f32 = jnp.bfloat16, jnp.float32
    gathered, mix, done, fresh = pl.pallas_call(
        functools.partial(kernel, n, axes),
        out_shape=(
            jax.ShapeDtypeStruct((layers, rows, cols), bf16),
            jax.ShapeDtypeStruct((rows, rows), f32),
            jax.ShapeDtypeStruct((layers - 1, rows, cols), bf16),
            jax.ShapeDtypeStruct((layers, rows, width), f32),
        ),
        in_specs=[any_spec, any_spec],
        out_specs=(vmem_spec, vmem_spec, vmem_spec, vmem_spec),
        scratch_shapes=[
            pltpu.VMEM((layers, rows, cols), bf16),
            pltpu.VMEM((layers, rows, width), f32),
            pltpu.VMEM((messages, rows, TILE), bf16),
            pltpu.VMEM((messages, rows, TILE), bf16),
            pltpu.VMEM((layers, rows, rows), f32),
            pltpu.VMEM((2, layers, 1, TILE), f32),
            pltpu.VMEM((layers, plane, 1, TILE), f32),
            pltpu.VMEM((layers, axes[0], 1, TILE), f32),
            dma((2,)),
            dma((messages,)),
            dma((messages,)),
            dma((messages,)),
            dma,
            dma,
            dma((layers,)),
            dma((layers,)),
            dma((layers, ring)),
            dma((layers, axes[0])),
        ],
        compiler_params=pltpu.CompilerParams(
            collective_id=0, has_side_effects=True, vmem_limit_bytes=40 * 1024 * 1024),
    )(pltpu.with_memory_space_constraint(pseudo_grads, pltpu.HBM),
      pltpu.with_memory_space_constraint(momentum, pltpu.HBM))
    return pl.pallas_call(
        finish,
        out_shape=(
            jax.ShapeDtypeStruct((layers, rows, cols), bf16),
            jax.ShapeDtypeStruct((layers, rows, width), f32),
        ),
        in_specs=[vmem_spec, vmem_spec, vmem_spec, vmem_spec],
        out_specs=(any_spec, any_spec),
        scratch_shapes=[
            pltpu.VMEM((rows, cols), bf16),
            dma((2 + PIECES,)),
        ],
        compiler_params=pltpu.CompilerParams(vmem_limit_bytes=40 * 1024 * 1024),
    )(gathered, mix, done, fresh)


def solution(mesh, axes=SHARD_AXES):
    placed = (P("replica", None, "shard", None), P(None, "shard", "replica"))
    return jax.shard_map(
        functools.partial(body, axes),
        mesh=mesh,
        in_specs=placed,
        out_specs=(P(None, "shard", None), P(None, "shard", "replica")),
        check_vma=False,
    )
```
